512 devices in a mesh: loop: 16 (over x, y_lo, core), groups: 32 (over y_hi, z).
Axes of the slice: x: 4, y: 8 (y_hi: 4, y_lo: 2; y = y_hi * 2 + y_lo), z: 8, core: 2. Of those that a mesh axis runs over, the one named last changes fastest.
Arguments:
- states: bfloat16 [65536, 1024], P(('loop', 'groups')), may hold values from -64 to 64
- premises: bfloat16 [65536, 1024], P(('loop', 'groups')), may hold values from -1 to 1
- counts: int32 [16, 32], P('loop', 'groups'), may hold values from 64 to 128, as said below
- partner_mask: int32 [16], P('loop'), may hold values from 0 to 31, as said below
- send_rows: int32 [16, 32, 16], P('loop', 'groups'), may hold values from 0 to 63
- hard_idx: int32 [65536], P(('loop', 'groups')), may hold values from 0 to 15
Outputs:
- loss: float32 [], replicated
- grad_states: bfloat16 [65536, 1024], P(('loop', 'groups'))
- grad_premises: bfloat16 [65536, 1024], P(('loop', 'groups'))
The draws below stay inside these ranges and needn't reach their ends.
Inputs may be any that keep to these rules, and one draw needn't show every extreme that they name: `counts`: at least 64 valid pairs on every device; some device has all slots valid. `partner_mask`: loop index 0 has the value 32 // 2.
All inputs are finite; a program needn't handle non-finite values.
Results may differ from the reference program's by a relative error of at most 0.0034.
Values may be sent and summed in bfloat16 or wider, within the bound.
A program may use at most 64 MiB of HBM per device.

```python
import jax
import jax.numpy as jnp
from jax import lax

D = 1024
TOK_DEV = 128
HARD = 16
PAIRS = 65536
N_LOOP = 16
N_GROUPS = 32


def pair_fields(key):
    key_a, key_b = jax.random.split(jax.random.fold_in(key, 11))
    prem = jnp.clip(jax.random.normal(key_a, (PAIRS, D), jnp.float32), -6.0, 6.0) * D ** (-0.5)
    stat = jnp.clip(jax.random.normal(key_b, (PAIRS, D), jnp.float32), -6.0, 6.0)
    return (stat, prem)


def draw_states(key, part):
    return pair_fields(key)[0].astype(jnp.bfloat16)


def draw_premises(key, part):
    return pair_fields(key)[1].astype(jnp.bfloat16)


def draw_counts(key, part):
    key_a, key_b = jax.random.split(jax.random.fold_in(key, 5))
    drawn = jax.random.randint(key_a, (N_LOOP * N_GROUPS,), TOK_DEV // 2, TOK_DEV + 1)
    where_full = jax.random.randint(key_b, (), 0, N_LOOP * N_GROUPS)
    drawn = drawn.at[where_full].set(TOK_DEV)
    return drawn.reshape(N_LOOP, N_GROUPS).astype(jnp.int32)


def draw_partner_mask(key, part):
    drawn = jax.random.randint(jax.random.fold_in(key, 23), (N_LOOP,), 0, N_GROUPS)
    drawn = drawn.at[0].set(N_GROUPS // 2)
    return drawn.astype(jnp.int32)


def touch_ends(values, rng, low, largest):
    spot = [jax.random.randint(jax.random.fold_in(rng, axis), (), 0, length) for axis, length in enumerate(values.shape)]
    widest = values.shape.index(max(values.shape))
    neighbour = spot[:widest] + [(spot[widest] + 1) % values.shape[widest]] + spot[widest + 1:]
    return values.at[tuple(spot)].set(low).at[tuple(neighbour)].set(largest)


def setup_inputs(seed: int = 0) -> dict:
    arg_keys = jax.random.split(jax.random.key(seed), 7)
    states = draw_states(jax.random.fold_in(arg_keys[6], 71), 0)
    premises = draw_premises(jax.random.fold_in(arg_keys[6], 71), 0)
    counts = draw_counts(jax.random.fold_in(arg_keys[6], 71), 0)
    partner_mask = draw_partner_mask(jax.random.fold_in(arg_keys[6], 71), 0)
    send_rows = touch_ends(jax.random.randint(arg_keys[4], (N_LOOP, N_GROUPS, HARD), 0, TOK_DEV // 2), jax.random.fold_in(arg_keys[4], 1), 0, (TOK_DEV // 2) - 1).astype(jnp.int32)
    hard_idx = touch_ends(jax.random.randint(arg_keys[5], (PAIRS,), 0, HARD), jax.random.fold_in(arg_keys[5], 1), 0, HARD - 1).astype(jnp.int32)
    return dict(states=states, premises=premises, counts=counts, partner_mask=partner_mask, send_rows=send_rows, hard_idx=hard_idx)


SCALE = 3.0


def reference(states, premises, counts, partner_mask, send_rows, hard_idx):
    width = states.shape[1]
    sfull = states.reshape(N_LOOP, N_GROUPS, TOK_DEV, width)
    qfull = premises.reshape(N_LOOP, N_GROUPS, TOK_DEV, width)
    index = hard_idx.reshape(N_LOOP, N_GROUPS, TOK_DEV)
    valid = jnp.arange(TOK_DEV, dtype=jnp.int32)[None, None, :] < counts[:, :, None]
    vflt = valid.astype(jnp.float32)
    gidx = jnp.arange(N_GROUPS, dtype=jnp.int32)
    partner = jnp.bitwise_xor(gidx[None, :], partner_mask[:, None]).astype(jnp.int32)
    offered = jnp.take_along_axis(qfull, send_rows[:, :, :, None], axis=2)
    pool = jnp.take_along_axis(offered, partner[:, :, None, None], axis=1)
    hard = jnp.take_along_axis(pool, index[:, :, :, None], axis=2)
    tval = SCALE * jnp.sum(sfull.astype(jnp.float32) * hard.astype(jnp.float32), axis=-1)

    sgrp = jnp.transpose(sfull, (1, 0, 2, 3)).reshape(N_GROUPS, N_LOOP * TOK_DEV, width)
    qgrp = jnp.transpose(qfull, (1, 0, 2, 3)).reshape(N_GROUPS, N_LOOP * TOK_DEV, width)
    vgrp = jnp.transpose(valid, (1, 0, 2)).reshape(N_GROUPS, N_LOOP * TOK_DEV)

    def one_group(item):
        sg, qg, vg = item
        scores = SCALE * jnp.dot(sg, qg.T, preferred_element_type=jnp.float32)
        masked = jnp.where(vg[None, :], scores, -jnp.inf)
        top = jnp.max(masked, axis=1)
        lse = top + jnp.log(jnp.sum(jnp.exp(masked - top[:, None]), axis=1))
        pos = jnp.diagonal(scores)
        prob = jnp.where(vg[:, None], jnp.exp(masked - lse[:, None]), 0.0).astype(jnp.bfloat16)
        dstate = jnp.dot(prob, qg, preferred_element_type=jnp.float32)
        dprem = jnp.dot(prob.T, sg, preferred_element_type=jnp.float32)
        return lse, pos, dstate, dprem

    lse, pos, dstate, dprem = lax.map(one_group, (sgrp, qgrp, vgrp))

    def regroup(arr):
        shaped = arr.reshape((N_GROUPS, N_LOOP, TOK_DEV) + arr.shape[2:])
        return jnp.swapaxes(shaped, 0, 1)

    lse = regroup(lse)
    pos = regroup(pos)
    dstate = regroup(dstate)
    dprem = regroup(dprem)
    qval = jnp.where(valid, jax.nn.sigmoid(tval - pos), 0.0)
    terms = jnp.where(valid, lse - pos + jax.nn.softplus(tval - pos), 0.0)
    loss = jnp.sum(terms) / (N_LOOP * N_GROUPS * TOK_DEV)
    grad_states = SCALE * (dstate + qval[..., None] * hard.astype(jnp.float32)
                           - (vflt + qval)[..., None] * qfull.astype(jnp.float32))
    pick = jax.nn.one_hot(index, HARD, dtype=jnp.float32)
    back = SCALE * jnp.einsum("lgpk,lgpd->lgkd", pick, qval[..., None] * sfull.astype(jnp.float32),
                              precision=lax.Precision.HIGHEST)
    back_home = jnp.take_along_axis(back, partner[:, :, None, None], axis=1)
    place = jax.nn.one_hot(send_rows, TOK_DEV, dtype=jnp.float32)
    dhard = jnp.einsum("lgkp,lgkd->lgpd", place, back_home, precision=lax.Precision.HIGHEST)
    grad_premises = dprem - SCALE * (vflt + qval)[..., None] * sfull.astype(jnp.float32) + dhard
    total = N_LOOP * N_GROUPS * TOK_DEV
    return (loss,
            grad_states.reshape(total, width).astype(jnp.bfloat16),
            grad_premises.reshape(total, width).astype(jnp.bfloat16))
```

```python
import functools

import jax
import jax.numpy as jnp
from jax import lax
from jax.experimental import pallas as pl
from jax.experimental.pallas import tpu as pltpu
from jax.sharding import PartitionSpec as P

SCALE = 3.0
NX, NC, NZ, NY = 4, 4, 8, 4
F32 = jnp.float32
BF16 = jnp.bfloat16
NN = (((1,), (0,)), ((), ()))
NT = (((1,), (1,)), ((), ()))
TN = (((0,), (0,)), ((), ()))


def dot(a, b, dims, precision=None):
    return lax.dot_general(a, b, dims, preferred_element_type=F32, precision=precision)


def kernel(
    counts_ref, mask_ref, send_ref, hidx_ref, states_hbm, prem_hbm,
    loss_ref, gs_hbm, gp_hbm,
    sall, pall, cntx, cnty, zbuf, ybuf, byuf, bzuf,
    ebuf, ptbuf, stats, hardb, own_s, own_p,
    dsend, r1, rx, psend, rp, lossx, lossc, lossy, lossz, gsb, gpb,
    local_sem, xs, xr, ys, yr, cs, cr, zs, zr, ts, tr, rs, rr, ps, pr, ls, lr,
):
    rows, width = states_hbm.shape
    half = rows // 2
    offer = zbuf.shape[1]
    me = lax.axis_index("loop")
    g = lax.axis_index("groups")
    x, yc = me // NC, me % NC
    yh, z = g // NZ, g % NZ
    top, bot = pl.ds(0, half), pl.ds(half, half)

    def xdev(step):
        return {"loop": ((x + step) % NX) * NC + yc, "groups": g}

    def cdev(flip):
        y, c = yc // 2, yc % 2
        y = (y + flip // 2) % 2
        c = (c + flip % 2) % 2
        return {"loop": x * NC + y * 2 + c, "groups": g}

    def zdev(step):
        return {"loop": me, "groups": yh * NZ + (z + step) % NZ}

    def ydev(step):
        return {"loop": me, "groups": ((yh + step) % NY) * NZ + z}

    sent = []

    def send(src, dst, ssem, rsem, device):
        copy = pltpu.make_async_remote_copy(
            src_ref=src, dst_ref=dst, send_sem=ssem, recv_sem=rsem,
            device_id=device, device_id_type=pl.DeviceIdType.MESH,
        )
        copy.start()
        sent.append(copy)
        return copy

    def spread(buf, n, devs, ssem, rsem, base=0):
        return [
            send(buf.at[0], buf.at[n - i], ssem.at[base + i], rsem.at[base + n - i], devs(i))
            for i in range(1, n)
        ]

    def spread_xor(buf, ssem, rsem, base=0):
        return [
            send(buf.at[0], buf.at[i], ssem.at[base + i], rsem.at[base + i], cdev(i))
            for i in range(1, NC)
        ]

    def arrive(copies):
        for copy in copies:
            copy.wait_recv()

    load_p = pltpu.make_async_copy(prem_hbm, pall.at[0], local_sem.at[0])
    load_s = pltpu.make_async_copy(states_hbm, sall.at[0], local_sem.at[1])
    load_p.start()
    load_s.start()

    barrier = pltpu.get_barrier_semaphore()
    peers = [xdev(i) for i in range(1, NX)] + [cdev(i) for i in range(1, NC)]
    peers += [zdev(i) for i in range(1, NZ)] + [ydev(i) for i in range(1, NY)]
    for peer in peers:
        pl.semaphore_signal(barrier, inc=1, device_id=peer, device_id_type=pl.DeviceIdType.MESH)

    count = counts_ref[0, 0]
    mask = mask_ref[0]
    cntx[0] = jnp.full(cntx.shape[1:], count, jnp.int32)
    cnty[0] = jnp.full(cnty.shape[1:], count, jnp.int32)
    place = lax.broadcasted_iota(jnp.int32, (rows, offer), 0) == send_ref[...]
    place = place.astype(F32).astype(BF16)
    load_p.wait()
    zbuf[0] = dot(place, pall[0], TN).astype(BF16)
    load_s.wait()
    pl.semaphore_wait(barrier, len(peers))

    offers_z = spread(zbuf, NZ, zdev, zs, zr)
    right_a = send(sall.at[0, top], sall.at[3, top], xs.at[0], xr.at[0], xdev(1))
    left_a = send(sall.at[0, bot], sall.at[1, bot], xs.at[1], xr.at[1], xdev(3))
    over_a = send(pall.at[0, top], pall.at[2, top], ys.at[0], yr.at[0], cdev(2))
    over_b = send(pall.at[0, bot], pall.at[2, bot], ys.at[1], yr.at[1], cdev(2))
    right_b = send(sall.at[0, bot], sall.at[3, bot], xs.at[2], xr.at[2], xdev(1))
    left_b = send(sall.at[0, top], sall.at[1, top], xs.at[3], xr.at[3], xdev(3))
    twin = send(pall.at[0], pall.at[1], ys.at[2], yr.at[2], cdev(1))
    counts_x = spread(cntx, NX, xdev, cs, cr)
    counts_c = spread_xor(cnty, cs, cr, NX)

    states_f = sall[0].astype(F32)
    prem_f = pall[0].astype(F32)
    pos = SCALE * jnp.sum(states_f * prem_f, axis=1, keepdims=True)
    valid = lax.broadcasted_iota(jnp.int32, (rows, 1), 0) < count
    vflt = valid.astype(F32)

    right_a.wait_recv()
    fwd_r = send(sall.at[3, top], sall.at[2, top], xs.at[4], xr.at[4], xdev(1))
    left_a.wait_recv()
    fwd_l = send(sall.at[1, bot], sall.at[2, bot], xs.at[5], xr.at[5], xdev(3))
    over_a.wait_recv()
    twin_a = send(pall.at[2, top], pall.at[3, top], ys.at[3], yr.at[3], cdev(1))
    over_b.wait_recv()
    twin_b = send(pall.at[2, bot], pall.at[3, bot], ys.at[4], yr.at[4], cdev(1))

    mz, my = mask % NZ, mask // NZ
    pick_z = ((z ^ mz) + NZ - z) % NZ
    pick_y = ((yh ^ my) + NY - yh) % NY

    arrive(offers_z)
    ybuf[0] = zbuf[pick_z]
    offers_y = spread(ybuf, NY, ydev, zs, zr, NZ)

    arrive([right_b, left_b, twin, twin_a, twin_b] + counts_x + counts_c)
    key = lax.broadcasted_iota(jnp.int32, (rows, rows), 0)
    keys_ok = [key < cnty[b, 0:1] for b in range(NC)]
    row = lax.broadcasted_iota(jnp.int32, (1, rows), 1)

    def scores(a):
        block = SCALE * dot(pall[...].reshape(NC * rows, width), sall[a], NT)
        parts = [
            jnp.where(keys_ok[b], block[b * rows:(b + 1) * rows], -jnp.inf) for b in range(NC)
        ]
        tops = [jnp.max(part, axis=0, keepdims=True) for part in parts]
        best = jnp.maximum(jnp.maximum(tops[0], tops[1]), jnp.maximum(tops[2], tops[3]))
        total = jnp.zeros((1, rows), F32)
        for b, part in enumerate(parts):
            part = jnp.exp(part - best)
            total = total + jnp.sum(part, axis=0, keepdims=True)
            ebuf[b * rows:(b + 1) * rows, a * rows:(a + 1) * rows] = part
        stats[0, a:a + 1] = best
        stats[0, NX + a:NX + a + 1] = total

    for a in (0, 1, 3):
        scores(a)
    arrive([fwd_r, fwd_l])
    scores(2)
    stats_x = spread(stats, NX, xdev, ts, tr)

    arrive(offers_y)
    pool = ybuf[pick_y]
    pick = lax.broadcasted_iota(jnp.int32, (offer, rows), 0) == hidx_ref[...]
    pick = pick.astype(F32)
    hard = dot(pick.astype(BF16), pool, TN)
    hardb[...] = hard.astype(BF16)
    states_f = sall[0].astype(F32)
    tval = SCALE * jnp.sum(states_f * hard, axis=1, keepdims=True)
    gap = tval - pos
    soft = jnp.maximum(gap, 0.0) + jnp.log1p(jnp.exp(-jnp.abs(gap)))
    qval = jnp.where(valid, jax.nn.sigmoid(gap), 0.0)
    back = SCALE * dot(pick, qval * states_f, NN, lax.Precision.HIGHEST)
    byuf[0] = back.astype(BF16)
    back_y = spread(byuf, NY, ydev, ts, tr, NX)

    arrive(stats_x)
    own_lse = None
    for a in range(NX):
        best = [stats[d, (a + NX - d) % NX:(a + NX - d) % NX + 1] for d in range(NX)]
        part = [stats[d, NX + (a + NX - d) % NX:NX + (a + NX - d) % NX + 1] for d in range(NX)]
        high = jnp.maximum(jnp.maximum(best[0], best[1]), jnp.maximum(best[2], best[3]))
        total = sum(part[d] * jnp.exp(best[d] - high) for d in range(NX))
        lse = high + jnp.log(total)
        if a == 0:
            own_lse = lse
        factor = jnp.where(row < cntx[a, 0:1], jnp.exp(best[0] - lse), 0.0)
        cols = slice(a * rows, (a + 1) * rows)
        ptbuf[:, cols] = (ebuf[:, cols] * factor).astype(BF16)

    loss = jnp.sum(jnp.where(row < count, own_lse, 0.0), axis=1, keepdims=True)
    loss = loss + jnp.sum(jnp.where(valid, soft - pos, 0.0), axis=0, keepdims=True)
    lossx[0] = jnp.broadcast_to(loss, lossx.shape[1:])
    loss_x = spread(lossx, NX, xdev, ls, lr)

    def dprem(b):
        return dot(ptbuf[b * rows:(b + 1) * rows], sall[...].reshape(NX * rows, width), NN)

    def dstate(a):
        return dot(ptbuf[:, a * rows:(a + 1) * rows], pall[...].reshape(NC * rows, width), TN)

    psend[2] = dprem(3).astype(BF16)
    via_twin = send(psend.at[2], rp.at[0], ps.at[0], pr.at[0], cdev(1))
    dsend[1] = dstate(2).astype(BF16)
    via_r = send(dsend.at[1, top], r1.at[0], rs.at[0], rr.at[0], xdev(1))
    via_l = send(dsend.at[1, bot], r1.at[1], rs.at[1], rr.at[1], xdev(3))
    dsend[0] = dstate(1).astype(BF16)
    lone_r = send(dsend.at[0, bot], rx.at[0, bot], rs.at[2], rr.at[2], xdev(1))
    dsend[2] = dstate(3).astype(BF16)
    lone_l = send(dsend.at[2, top], rx.at[1, top], rs.at[3], rr.at[3], xdev(3))
    over = dprem(2)
    via_twin.wait_recv()
    psend[1] = (over + rp[0].astype(F32)).astype(BF16)
    over_p = send(psend.at[1], rp.at[2], ps.at[2], pr.at[2], cdev(2))
    psend[0] = dprem(1).astype(BF16)
    twin_p = send(psend.at[0], rp.at[1], ps.at[1], pr.at[1], cdev(1))
    via_r.wait_recv()
    dsend[0, top] = (dsend[0, top].astype(F32) + r1[0].astype(F32)).astype(BF16)
    pair_r = send(dsend.at[0, top], rx.at[0, top], rs.at[4], rr.at[4], xdev(1))
    via_l.wait_recv()
    dsend[2, bot] = (dsend[2, bot].astype(F32) + r1[1].astype(F32)).astype(BF16)
    pair_l = send(dsend.at[2, bot], rx.at[1, bot], rs.at[5], rr.at[5], xdev(3))
    own_s[...] = dstate(0)
    own_p[...] = dprem(0)

    arrive(loss_x)
    lossc[0] = lossx[0] + lossx[1] + lossx[2] + lossx[3]
    loss_c = spread_xor(lossc, ls, lr, NX)

    arrive(back_y)
    bzuf[0] = byuf[pick_y]
    back_z = spread(bzuf, NZ, zdev, ts, tr, NX + NY)

    arrive(loss_c)
    lossy[0] = lossc[0] + lossc[1] + lossc[2] + lossc[3]
    loss_y = spread(lossy, NY, ydev, ls, lr, NX + NC)

    weight = vflt + qval
    arrive([lone_r, lone_l, pair_r, pair_l])
    dstates = own_s[...] + rx[0].astype(F32) + rx[1].astype(F32)
    dstates = dstates + qval * hardb[...].astype(F32) - weight * pall[0].astype(F32)
    gsb[...] = (SCALE * dstates).astype(BF16)
    put_s = pltpu.make_async_copy(gsb, gs_hbm, local_sem.at[2])
    put_s.start()

    arrive(loss_y)
    lossz[0] = lossy[0] + lossy[1] + lossy[2] + lossy[3]
    loss_z = spread(lossz, NZ, zdev, ls, lr, NX + NC + NY)

    arrive([over_p, twin_p])
    dprems = own_p[...] + rp[1].astype(F32) + rp[2].astype(F32)
    own_p[...] = dprems - SCALE * weight * sall[0].astype(F32)

    arrive(back_z)
    home = bzuf[pick_z]
    gpb[...] = (own_p[...] + dot(place, home, NN)).astype(BF16)
    put_p = pltpu.make_async_copy(gpb, gp_hbm, local_sem.at[3])
    put_p.start()

    arrive(loss_z)
    full = lossz[0]
    for i in range(1, NZ):
        full = full + lossz[i]
    loss_ref[...] = full[0:1, 0:1] / (NX * NC * NZ * NY * rows)

    for copy in sent:
        copy.wait_send()
    put_s.wait()
    put_p.wait()


def body(states, premises, counts, partner_mask, send_rows, hard_idx):
    rows, width = states.shape
    offer = send_rows.shape[2]
    vmem = pltpu.VMEM
    dma = pltpu.SemaphoreType.DMA
    any_spec = pl.BlockSpec(memory_space=pl.ANY)
    vmem_spec = pl.BlockSpec(memory_space=pltpu.VMEM)
    smem_spec = pl.BlockSpec(memory_space=pltpu.SMEM)
    loss, gs, gp = pl.pallas_call(
        kernel,
        out_shape=(
            jax.ShapeDtypeStruct((1, 1), F32),
            jax.ShapeDtypeStruct((rows, width), BF16),
            jax.ShapeDtypeStruct((rows, width), BF16),
        ),
        in_specs=[smem_spec, smem_spec, vmem_spec, vmem_spec, any_spec, any_spec],
        out_specs=(vmem_spec, any_spec, any_spec),
        scratch_shapes=[
            vmem((NX, rows, width), BF16),
            vmem((NC, rows, width), BF16),
            vmem((NX, 8, rows), jnp.int32),
            vmem((NC, 8, rows), jnp.int32),
            vmem((NZ, offer, width), BF16),
            vmem((NY, offer, width), BF16),
            vmem((NY, offer, width), BF16),
            vmem((NZ, offer, width), BF16),
            vmem((NC * rows, NX * rows), F32),
            vmem((NC * rows, NX * rows), BF16),
            vmem((NX, 2 * NX, rows), F32),
            vmem((rows, width), BF16),
            vmem((rows, width), F32),
            vmem((rows, width), F32),
            vmem((3, rows, width), BF16),
            vmem((2, rows // 2, width), BF16),
            vmem((2, rows, width), BF16),
            vmem((3, rows, width), BF16),
            vmem((3, rows, width), BF16),
            vmem((NX, 8, 128), F32),
            vmem((NC, 8, 128), F32),
            vmem((NY, 8, 128), F32),
            vmem((NZ, 8, 128), F32),
            vmem((rows, width), BF16),
            vmem((rows, width), BF16),
            dma((4,)),
            dma((6,)), dma((6,)),
            dma((5,)), dma((5,)),
            dma((NX + NC,)), dma((NX + NC,)),
            dma((NZ + NY,)), dma((NZ + NY,)),
            dma((NX + NY + NZ,)), dma((NX + NY + NZ,)),
            dma((6,)), dma((6,)),
            dma((3,)), dma((3,)),
            dma((NX + NC + NY + NZ,)), dma((NX + NC + NY + NZ,)),
        ],
        compiler_params=pltpu.CompilerParams(collective_id=0, has_side_effects=True),
    )(
        counts,
        partner_mask,
        send_rows.reshape(1, offer),
        hard_idx.reshape(1, rows),
        states,
        premises,
    )
    return loss.reshape(()), gs, gp


def solution(mesh):
    return jax.shard_map(
        body,
        mesh=mesh,
        in_specs=(
            P(("loop", "groups"), None),
            P(("loop", "groups"), None),
            P("loop", "groups"),
            P("loop"),
            P("loop", "groups", None),
            P(("loop", "groups")),
        ),
        out_specs=(P(), P(("loop", "groups"), None), P(("loop", "groups"), None)),
        check_vma=False,
    )
```

```python
import functools

import jax
import jax.numpy as jnp
from jax import lax
from jax.experimental import pallas as pl
from jax.experimental.pallas import tpu as pltpu
from jax.sharding import PartitionSpec as P

SCALE = 3.0
NX, NC, NZ, NY = 4, 4, 8, 4
F32 = jnp.float32
BF16 = jnp.bfloat16
NN = (((1,), (0,)), ((), ()))
NT = (((1,), (1,)), ((), ()))
TN = (((0,), (0,)), ((), ()))


def dot(a, b, dims, precision=None):
    return lax.dot_general(a, b, dims, preferred_element_type=F32, precision=precision)


def kernel(
    counts_ref, mask_ref, send_hbm, hidx_hbm, states_hbm, prem_hbm,
    loss_ref, gs_ref, gp_ref,
    send_ref, hidx_ref,
    sall, pall, cntx, cnty, zbuf, ybuf, byuf, bzuf,
    ebuf, ptbuf, stats, hardb, own_s, own_p,
    dsend, r1, rx, psend, rp, lossg, lossy, lossz,
    local_sem, xs, xr, ys, yr, cs, cr, zs, zr, ts, tr, rs, rr, ps, pr, ls, lr,
):
    rows, width = states_hbm.shape
    half = rows // 2
    offer = zbuf.shape[1]
    me = lax.axis_index("loop")
    g = lax.axis_index("groups")
    x, yc = me // NC, me % NC
    yh, z = g // NZ, g % NZ
    top, bot = pl.ds(0, half), pl.ds(half, half)

    def xdev(step):
        return {"loop": ((x + step) % NX) * NC + yc, "groups": g}

    def cdev(flip):
        y, c = yc // 2, yc % 2
        y = (y + flip // 2) % 2
        c = (c + flip % 2) % 2
        return {"loop": x * NC + y * 2 + c, "groups": g}

    def gdev(step, flip):
        y, c = yc // 2, yc % 2
        y = (y + flip // 2) % 2
        c = (c + flip % 2) % 2
        return {"loop": ((x + step) % NX) * NC + y * 2 + c, "groups": g}

    def zdev(step):
        return {"loop": me, "groups": yh * NZ + (z + step) % NZ}

    def ydev(step):
        return {"loop": me, "groups": ((yh + step) % NY) * NZ + z}

    sent = []

    def send(src, dst, ssem, rsem, device):
        copy = pltpu.make_async_remote_copy(
            src_ref=src, dst_ref=dst, send_sem=ssem, recv_sem=rsem,
            device_id=device, device_id_type=pl.DeviceIdType.MESH,
        )
        copy.start()
        sent.append(copy)
        return copy

    def spread(buf, n, devs, ssem, rsem, base=0):
        order = sorted(range(1, n), key=lambda i: -min(i, n - i))
        return [
            send(buf.at[0], buf.at[n - i], ssem.at[base + i], rsem.at[base + n - i], devs(i))
            for i in order
        ]

    def spread_xor(buf, ssem, rsem, base=0):
        return [
            send(buf.at[0], buf.at[i], ssem.at[base + i], rsem.at[base + i], cdev(i))
            for i in range(1, NC)
        ]

    def arrive(copies):
        for copy in copies:
            copy.wait_recv()

    barrier = pltpu.get_barrier_semaphore()
    mates = [(i, j) for i in range(NX) for j in range(NC) if i or j]
    peers = [zdev(i) for i in (4, 3, 5, 2, 6, 1, 7)] + [ydev(i) for i in (2, 1, 3)]
    peers += [gdev(i, j) for i, j in mates]
    for peer in peers:
        pl.semaphore_signal(barrier, inc=1, device_id=peer, device_id_type=pl.DeviceIdType.MESH)
    pairs = [
        (prem_hbm, pall.at[0]), (send_hbm, send_ref), (states_hbm, sall.at[0]),
        (hidx_hbm, hidx_ref),
    ]
    loads = [pltpu.make_async_copy(a, b, local_sem.at[i]) for i, (a, b) in enumerate(pairs)]
    for load in loads:
        load.start()
    loads[0].wait()
    loads[1].wait()
    place = lax.broadcasted_iota(jnp.int32, (rows, offer), 0) == send_ref[...]
    place = place.astype(F32).astype(BF16)
    zbuf[0] = dot(place, pall[0], TN).astype(BF16)
    for load in loads[2:]:
        load.wait()

    count = counts_ref[0, 0]
    mask = mask_ref[0]
    cntx[0] = jnp.full(cntx.shape[1:], count, jnp.int32)
    cnty[0] = jnp.full(cnty.shape[1:], count, jnp.int32)
    pl.semaphore_wait(barrier, len(peers))

    offers_z = spread(zbuf, NZ, zdev, zs, zr)
    right_a = send(sall.at[0, top], sall.at[3, top], xs.at[0], xr.at[0], xdev(1))
    left_a = send(sall.at[0, bot], sall.at[1, bot], xs.at[1], xr.at[1], xdev(3))
    over_a = send(pall.at[0, top], pall.at[2, top], ys.at[0], yr.at[0], cdev(2))
    over_b = send(pall.at[0, bot], pall.at[2, bot], ys.at[1], yr.at[1], cdev(2))
    right_b = send(sall.at[0, bot], sall.at[3, bot], xs.at[2], xr.at[2], xdev(1))
    left_b = send(sall.at[0, top], sall.at[1, top], xs.at[3], xr.at[3], xdev(3))
    twin = send(pall.at[0], pall.at[1], ys.at[2], yr.at[2], cdev(1))
    counts_x = spread(cntx, NX, xdev, cs, cr)
    counts_c = spread_xor(cnty, cs, cr, NX)

    states_f = sall[0].astype(F32)
    prem_f = pall[0].astype(F32)
    pos = SCALE * jnp.sum(states_f * prem_f, axis=1, keepdims=True)
    valid = lax.broadcasted_iota(jnp.int32, (rows, 1), 0) < count
    vflt = valid.astype(F32)

    right_a.wait_recv()
    fwd_r = send(sall.at[3, top], sall.at[2, top], xs.at[4], xr.at[4], xdev(1))
    left_a.wait_recv()
    fwd_l = send(sall.at[1, bot], sall.at[2, bot], xs.at[5], xr.at[5], xdev(3))
    over_a.wait_recv()
    twin_a = send(pall.at[2, top], pall.at[3, top], ys.at[3], yr.at[3], cdev(1))
    over_b.wait_recv()
    twin_b = send(pall.at[2, bot], pall.at[3, bot], ys.at[4], yr.at[4], cdev(1))

    mz, my = mask % NZ, mask // NZ
    pick_z = ((z ^ mz) + NZ - z) % NZ
    pick_y = ((yh ^ my) + NY - yh) % NY

    arrive(offers_z)
    ybuf[0] = zbuf[pick_z]
    offers_y = spread(ybuf, NY, ydev, zs, zr, NZ)

    arrive([right_b, left_b, twin, twin_a, twin_b] + counts_x + counts_c)
    key = lax.broadcasted_iota(jnp.int32, (rows, rows), 0)
    keys_ok = [key < cnty[b, 0:1] for b in range(NC)]
    row = lax.broadcasted_iota(jnp.int32, (1, rows), 1)

    def scores(a):
        block = SCALE * dot(pall[...].reshape(NC * rows, width), sall[a], NT)
        parts = [
            jnp.where(keys_ok[b], block[b * rows:(b + 1) * rows], -jnp.inf) for b in range(NC)
        ]
        tops = [jnp.max(part, axis=0, keepdims=True) for part in parts]
        best = jnp.maximum(jnp.maximum(tops[0], tops[1]), jnp.maximum(tops[2], tops[3]))
        total = jnp.zeros((1, rows), F32)
        for b, part in enumerate(parts):
            part = jnp.exp(part - best)
            total = total + jnp.sum(part, axis=0, keepdims=True)
            ebuf[b * rows:(b + 1) * rows, a * rows:(a + 1) * rows] = part
        stats[0, a:a + 1] = best
        stats[0, NX + a:NX + a + 1] = total

    for a in (0, 1, 3):
        scores(a)
    arrive([fwd_r, fwd_l])
    scores(2)
    stats_x = spread(stats, NX, xdev, ts, tr)

    arrive(offers_y)
    pool = ybuf[pick_y]
    pick = lax.broadcasted_iota(jnp.int32, (offer, rows), 0) == hidx_ref[...]
    pick = pick.astype(F32)
    hard = dot(pick.astype(BF16), pool, TN)
    hardb[...] = hard.astype(BF16)
    states_f = sall[0].astype(F32)
    tval = SCALE * jnp.sum(states_f * hard, axis=1, keepdims=True)
    gap = tval - pos
    soft = jnp.maximum(gap, 0.0) + jnp.log1p(jnp.exp(-jnp.abs(gap)))
    qval = jnp.where(valid, jax.nn.sigmoid(gap), 0.0)
    back = SCALE * dot(pick, qval * states_f, NN, lax.Precision.HIGHEST)
    byuf[0] = back.astype(BF16)
    back_y = spread(byuf, NY, ydev, ts, tr, NX)

    arrive(stats_x)
    own_lse = None
    for a in range(NX):
        best = [stats[d, (a + NX - d) % NX:(a + NX - d) % NX + 1] for d in range(NX)]
        part = [stats[d, NX + (a + NX - d) % NX:NX + (a + NX - d) % NX + 1] for d in range(NX)]
        high = jnp.maximum(jnp.maximum(best[0], best[1]), jnp.maximum(best[2], best[3]))
        total = sum(part[d] * jnp.exp(best[d] - high) for d in range(NX))
        lse = high + jnp.log(total)
        if a == 0:
            own_lse = lse
        factor = jnp.where(row < cntx[a, 0:1], jnp.exp(best[0] - lse), 0.0)
        cols = slice(a * rows, (a + 1) * rows)
        ptbuf[:, cols] = (ebuf[:, cols] * factor).astype(BF16)

    loss = jnp.sum(jnp.where(row < count, own_lse, 0.0), axis=1, keepdims=True)
    loss = loss + jnp.sum(jnp.where(valid, soft - pos, 0.0), axis=0, keepdims=True)
    lossg[0] = jnp.broadcast_to(loss, lossg.shape[1:])
    loss_g = []
    for i, j in mates:
        to, here = i * NC + j, (NX - i) % NX * NC + j
        loss_g.append(send(lossg.at[0], lossg.at[here], ls.at[to], lr.at[here], gdev(i, j)))

    def dprem(b):
        return dot(ptbuf[b * rows:(b + 1) * rows], sall[...].reshape(NX * rows, width), NN)

    def dstate(a):
        return dot(ptbuf[:, a * rows:(a + 1) * rows], pall[...].reshape(NC * rows, width), TN)

    psend[2] = dprem(3).astype(BF16)
    via_twin = send(psend.at[2], rp.at[0], ps.at[0], pr.at[0], cdev(1))
    dsend[1] = dstate(2).astype(BF16)
    via_r = send(dsend.at[1, top], r1.at[0], rs.at[0], rr.at[0], xdev(1))
    via_l = send(dsend.at[1, bot], r1.at[1], rs.at[1], rr.at[1], xdev(3))
    dsend[0] = dstate(1).astype(BF16)
    lone_r = send(dsend.at[0, bot], rx.at[0, bot], rs.at[2], rr.at[2], xdev(1))
    dsend[2] = dstate(3).astype(BF16)
    lone_l = send(dsend.at[2, top], rx.at[1, top], rs.at[3], rr.at[3], xdev(3))
    over = dprem(2)
    via_twin.wait_recv()
    psend[1] = (over + rp[0].astype(F32)).astype(BF16)
    over_p = send(psend.at[1], rp.at[2], ps.at[2], pr.at[2], cdev(2))
    psend[0] = dprem(1).astype(BF16)
    twin_p = send(psend.at[0], rp.at[1], ps.at[1], pr.at[1], cdev(1))
    own_s[...] = dstate(0)
    own_p[...] = dprem(0)
    weight = vflt + qval
    own_s[...] += qval * hardb[...].astype(F32) - weight * pall[0].astype(F32)
    own_p[...] -= SCALE * weight * sall[0].astype(F32)

    arrive(back_y)
    bzuf[0] = byuf[pick_y]
    back_z = spread(bzuf, NZ, zdev, ts, tr, NX + NY)

    def total(buf):
        value = buf[0]
        for i in range(1, buf.shape[0]):
            value = value + buf[i]
        return value

    arrive(loss_g)
    lossy[0] = total(lossg)
    loss_y = spread(lossy, NY, ydev, ls, lr, NX * NC)

    via_r.wait_recv()
    dsend[0, top] = (dsend[0, top].astype(F32) + r1[0].astype(F32)).astype(BF16)
    pair_r = send(dsend.at[0, top], rx.at[0, top], rs.at[4], rr.at[4], xdev(1))
    via_l.wait_recv()
    dsend[2, bot] = (dsend[2, bot].astype(F32) + r1[1].astype(F32)).astype(BF16)
    pair_l = send(dsend.at[2, bot], rx.at[1, bot], rs.at[5], rr.at[5], xdev(3))

    arrive(loss_y)
    lossz[0] = total(lossy)
    loss_z = spread(lossz, NZ, zdev, ls, lr, NX * NC + NY)

    arrive([over_p, twin_p])
    own_p[...] += rp[1].astype(F32) + rp[2].astype(F32)

    arrive([lone_r, lone_l, pair_r, pair_l])
    dstates = own_s[...] + rx[0].astype(F32) + rx[1].astype(F32)
    gs_ref[...] = (SCALE * dstates).astype(BF16)

    arrive(back_z)
    home = bzuf[pick_z]
    gp_ref[...] = (own_p[...] + dot(place, home, NN)).astype(BF16)

    arrive(loss_z)
    loss_ref[...] = total(lossz) / (NX * NC * NZ * NY * rows)

    for copy in sent:
        copy.wait_send()


def flush(loss_ref, gs_ref, gp_ref, loss_out, gs_out, gp_out, sem):
    put_s = pltpu.make_async_copy(gs_ref, gs_out, sem.at[0])
    put_p = pltpu.make_async_copy(gp_ref, gp_out, sem.at[1])
    put_s.start()
    put_p.start()
    loss_out[...] = loss_ref[0:1, 0:1]
    put_s.wait()
    put_p.wait()


def body(states, premises, counts, partner_mask, send_rows, hard_idx):
    rows, width = states.shape
    offer = send_rows.shape[2]
    vmem = pltpu.VMEM
    dma = pltpu.SemaphoreType.DMA
    any_spec = pl.BlockSpec(memory_space=pl.ANY)
    vmem_spec = pl.BlockSpec(memory_space=pltpu.VMEM)
    smem_spec = pl.BlockSpec(memory_space=pltpu.SMEM)
    loss, gs, gp = pl.pallas_call(
        kernel,
        out_shape=(vmem((8, 128), F32), vmem((rows, width), BF16), vmem((rows, width), BF16)),
        in_specs=[smem_spec] * 2 + [any_spec] * 4,
        out_specs=(vmem_spec,) * 3,
        scratch_shapes=[
            vmem((1, offer), jnp.int32),
            vmem((1, rows), jnp.int32),
            vmem((NX, rows, width), BF16),
            vmem((NC, rows, width), BF16),
            vmem((NX, 8, rows), jnp.int32),
            vmem((NC, 8, rows), jnp.int32),
            vmem((NZ, offer, width), BF16),
            vmem((NY, offer, width), BF16),
            vmem((NY, offer, width), BF16),
            vmem((NZ, offer, width), BF16),
            vmem((NC * rows, NX * rows), F32),
            vmem((NC * rows, NX * rows), BF16),
            vmem((NX, 2 * NX, rows), F32),
            vmem((rows, width), BF16),
            vmem((rows, width), F32),
            vmem((rows, width), F32),
            vmem((3, rows, width), BF16),
            vmem((2, rows // 2, width), BF16),
            vmem((2, rows, width), BF16),
            vmem((3, rows, width), BF16),
            vmem((3, rows, width), BF16),
            vmem((NX * NC, 8, 128), F32),
            vmem((NY, 8, 128), F32),
            vmem((NZ, 8, 128), F32),
            dma((4,)),
            dma((6,)), dma((6,)),
            dma((5,)), dma((5,)),
            dma((NX + NC,)), dma((NX + NC,)),
            dma((NZ + NY,)), dma((NZ + NY,)),
            dma((NX + NY + NZ,)), dma((NX + NY + NZ,)),
            dma((6,)), dma((6,)),
            dma((3,)), dma((3,)),
            dma((NX * NC + NY + NZ,)), dma((NX * NC + NY + NZ,)),
        ],
        compiler_params=pltpu.CompilerParams(collective_id=0, has_side_effects=True),
    )(
        counts,
        partner_mask,
        send_rows.reshape(1, offer),
        hard_idx.reshape(1, rows),
        states,
        premises,
    )
    loss, gs, gp = pl.pallas_call(
        flush,
        out_shape=(
            jax.ShapeDtypeStruct((1, 1), F32),
            jax.ShapeDtypeStruct((rows, width), BF16),
            jax.ShapeDtypeStruct((rows, width), BF16),
        ),
        in_specs=[vmem_spec, any_spec, any_spec],
        out_specs=(vmem_spec, any_spec, any_spec),
        scratch_shapes=[dma((2,))],
        compiler_params=pltpu.CompilerParams(vmem_limit_bytes=2**20),
    )(loss, gs, gp)
    return loss.reshape(()), gs, gp


def solution(mesh):
    return jax.shard_map(
        body,
        mesh=mesh,
        in_specs=(
            P(("loop", "groups"), None),
            P(("loop", "groups"), None),
            P("loop", "groups"),
            P("loop"),
            P("loop", "groups", None),
            P(("loop", "groups")),
        ),
        out_specs=(P(), P(("loop", "groups"), None), P(("loop", "groups"), None)),
        check_vma=False,
    )
```
